32 devices in a mesh: groups: 2 (over x), tile: 16 (over z, y, core).
Axes of the slice: x: 2, y: 2, z: 4, core: 2. Of those that a mesh axis runs over, the one named last changes fastest.
Arguments:
- tiles: float32 [2, 12288, 384], P(None, ('groups', 'tile')), parts along dimension 1, may hold values from -6 to 6
- library: float32 [128, 2, 128, 128], P('tile'), may hold values from -6 to 6
- block_owner: int32 [2], replicated, may hold values from 0 to 15
- block_clips: int32 [2, 2], replicated, may hold values from 0 to 7
- layer_order: int32 [32, 2], P(('groups', 'tile')), parts along dimension 0, may hold values from 0 to 1, each once within a row
Outputs:
- scores: float32 [2, 2, 12288, 384], P(None, None, ('groups', 'tile')), parts along dimension 2
- peak_scores: float32 [4, 2], P('groups'), parts along dimension 0
The draws below stay inside these ranges and needn't reach their ends.
There are 2 independent parts, one for each index of `groups`. The reference program is written for one: setup_inputs(seed, part) draws one part's arguments, and reference() takes and returns one part's arrays. A program takes and returns all parts, laid end to end along the dimension named above; an argument that names none is the same for every part. Nothing has to cross between parts.
Inputs may be any that keep to these rules, and one draw needn't show every extreme that they name: `layer_order`: each row is a permutation of 0 to 1.
All inputs are finite; a program needn't handle non-finite values.
Results may differ from the reference program's by a relative error of at most 0.000098.
Values sent between devices are 32-bit elements; how exact they have to be, the bound alone decides.
A program may use at most 128 MiB of HBM per device.

```python
import math
import jax
import jax.numpy as jnp
from jax import lax

SPAN = 512
CLIP = 128
LAYERS = 2
CLIPS_DEV = 8
BLOCKS = 2
PER_BLOCK = 2
ROWS = 384
COLS = 384
TILES = 16
LIBRARY = 128


def place_ends(drawn, rng, low, top_value):
    place = [jax.random.randint(jax.random.fold_in(rng, axis), (), 0, length) for axis, length in enumerate(drawn.shape)]
    main_axis = drawn.shape.index(max(drawn.shape))
    neighbour = place[:main_axis] + [(place[main_axis] + 1) % drawn.shape[main_axis]] + place[main_axis + 1:]
    return drawn.at[tuple(place)].set(low).at[tuple(neighbour)].set(top_value)


def levels(key, shape, pieces, least, top_value):
    gain, own = 1.0, jax.random.fold_in(key, 6)
    for axis_at, parts in pieces:
        steps = jnp.exp(jax.random.uniform(jax.random.fold_in(own, axis_at), (parts,), jnp.float32, least / len(pieces), top_value / len(pieces)))
        gain = gain * jnp.repeat(steps, shape[axis_at] // parts).reshape([-1 if axis == axis_at else 1 for axis in range(len(shape))])
    return gain


def centred(stream_key, shape, width, most, split=(), held_as=jnp.bfloat16):
    drawn = width * jax.random.normal(stream_key, shape, jnp.float32)
    if split:
        drawn = drawn * levels(stream_key, shape, split, -0.22, 0.18)
    return jnp.clip(drawn, -most, most).astype(held_as)


def setup_inputs(seed: int = 0, part: int = 0) -> dict:
    seeds = jax.random.split(jax.random.key(seed), 6)
    own_keys = jax.random.split(jax.random.fold_in(seeds[5], part), 6)
    return {
        "tiles": centred(own_keys[0], (LAYERS, TILES * ROWS, COLS), 1.0, 6.0, ((1, 16),), jnp.float32),
        "library": centred(seeds[1], (LIBRARY, LAYERS, CLIP, CLIP), 1.0, 6.0, ((0, 16),), jnp.float32),
        "block_owner": jax.random.randint(seeds[2], (BLOCKS,), 0, TILES).astype(jnp.int32),
        "block_clips": place_ends(jax.random.randint(seeds[3], (BLOCKS, PER_BLOCK), 0, CLIPS_DEV), jax.random.fold_in(seeds[3], 1), 0, CLIPS_DEV - 1).astype(jnp.int32),
        "layer_order": jax.vmap(lambda own: jax.random.permutation(own, LAYERS))(jax.random.split(own_keys[4], TILES)).reshape((TILES, LAYERS)).astype(jnp.int32),
    }


def window_band(length, starts, extent, number_type):
    position = jnp.arange(length)[:, None]
    anchor = jnp.arange(starts)[None, :]
    offset = position - anchor
    return ((offset >= 0) & (offset < extent)).astype(number_type)

def reference(tiles, library, block_owner, block_clips, layer_order):
    chosen = (block_owner[:, None] * CLIPS_DEV + block_clips).reshape(-1).astype(jnp.int32)
    chosen_clips = library[chosen]
    clip_rms = jnp.sqrt(lax.optimization_barrier(jnp.mean(chosen_clips * chosen_clips, axis=(1, 2, 3))) + 1e-05)
    padded_clips = jnp.pad(chosen_clips, ((0, 0), (0, 0), (0, SPAN - CLIP), (0, SPAN - CLIP)))
    clip_spectra = jnp.conj(jnp.fft.fft2(padded_clips))
    strip_rows = tiles.reshape(LAYERS, TILES, ROWS, COLS)
    following = jnp.concatenate([strip_rows[:, 1:, :CLIP, :], jnp.zeros((LAYERS, 1, CLIP, COLS), tiles.dtype)], axis=1)
    extended = jnp.moveaxis(jnp.concatenate([strip_rows, following], axis=2), 1, 0)
    band_rows = window_band(SPAN, ROWS, CLIP, tiles.dtype)
    band_cols = window_band(COLS, COLS, CLIP, tiles.dtype)
    root_count = math.sqrt(LAYERS * CLIP * CLIP)

    def one_tile(inputs):
        tile_block, layer_pick = inputs
        padded = jnp.pad(tile_block, ((0, 0), (0, 0), (0, SPAN - COLS)))
        spectra = jnp.fft.fft2(padded)
        crossed = lax.optimization_barrier(jnp.sum(spectra[None] * clip_spectra[:, layer_pick], axis=1))
        correlation = jnp.real(jnp.fft.ifft2(crossed))[:, :ROWS, :COLS]
        squares = lax.optimization_barrier(jnp.sum(tile_block * tile_block, axis=0))
        energy = jnp.dot(jnp.dot(band_rows.T, squares, precision=lax.Precision.HIGHEST), band_cols, precision=lax.Precision.HIGHEST)
        window_rms = jnp.sqrt(energy / (LAYERS * CLIP * CLIP) + 1e-05)
        return correlation / (root_count * clip_rms[:, None, None] * window_rms[None])
    all_scores = lax.map(one_tile, (extended, layer_order))
    all_scores = jnp.moveaxis(all_scores, 1, 0).reshape(BLOCKS, PER_BLOCK, TILES * ROWS, COLS)
    peak_scores = lax.optimization_barrier(jnp.max(all_scores, axis=(2, 3)))
    return (all_scores, peak_scores)
```

```python
import functools
import math

import jax
import jax.numpy as jnp
import numpy as np
from jax import lax
from jax.experimental import pallas as pl
from jax.experimental.pallas import tpu as pltpu
from jax.sharding import PartitionSpec as P

F32 = jnp.float32
BF16 = jnp.bfloat16


def from_behind(block, axis):
    devices = range(lax.axis_size(axis))
    return lax.ppermute(block, axis, [(i + 1, i) for i in devices if i + 1 in devices])


def split(x):
    high = x.astype(BF16)
    return high, (x - high.astype(F32)).astype(BF16)


def mm(a, b):
    return jnp.dot(a, b, preferred_element_type=F32)


def transform_matrix(extent):
    span = 2 * extent
    odd = 2 * np.arange(extent)[:, None] + 1
    angle = (odd * np.arange(span)[None, :] % (2 * span)) * (math.pi / span)
    return np.concatenate([np.cos(angle), np.sin(angle)], axis=0).astype(np.float32)


def halves(matrix):
    high = matrix.astype(BF16)
    low = (matrix - high.astype(np.float32)).astype(BF16)
    return high, low


def constants(extent):
    forward = transform_matrix(extent)
    fh, fl = halves(forward)
    row_left = np.concatenate([fh, fl, fh], axis=1)
    ft = np.ascontiguousarray(forward.T)
    th, tl = halves(ft)
    col_right = np.stack([th, tl])
    back = forward[:, :extent] * np.float32(1.0 / extent)
    bh, bl = halves(back)
    back_right = np.stack([bh, bl])
    back_left = np.concatenate([bh.T, bl.T, bh.T], axis=1)
    offset = np.arange(2 * extent)[None, :] - np.arange(extent)[:, None]
    band = ((offset >= 0) & (offset < extent)).astype(BF16)
    band_left = np.concatenate([band, band], axis=1)
    band_right = np.ascontiguousarray(band.T)
    return [jnp.asarray(c) for c in (row_left, col_right, back_left, back_right, band_left, band_right)]


def combine(y, e):
    a, b = y[:e, :e], y[:e, e:]
    c, d = y[e:, :e], y[e:, e:]
    return a - d, b + c, a + d, c - b


def kernel(order, tiles, halo, clips, row_left, col_right, back_left, back_right, band_left, band_right,
           scores, peaks, yh, yl, inv, spectra, wh, wl):
    layers, rows, cols = tiles.shape
    blocks, per_block = clips.shape[:2]
    count = blocks * per_block
    e = clips.shape[-1]
    span = 2 * e
    nr, nc = rows // e, cols // e
    entries = layers * e * e

    clip_scale = []
    for k in range(count):
        total = jnp.zeros((e, e), F32)
        for l in range(layers):
            chosen = clips[k // per_block, k % per_block, order[0, l]]
            total = total + chosen * chosen
            ch, cl = split(chosen)
            first = mm(row_left[:, :e], ch) + mm(row_left[:, span:span + e], ch) + mm(row_left[:, :e], cl)
            fh, fl = split(first)
            second = mm(fh, col_right[0, :e]) + mm(fl, col_right[0, :e]) + mm(fh, col_right[1, :e])
            for n, part in enumerate(combine(second, e)):
                spectra[k, l, n] = part
        mean = jnp.sum(total, keepdims=True) / entries
        clip_scale.append(1.0 / (math.sqrt(entries) * jnp.sqrt(mean + 1e-05)))

    for b in range(nr):
        squares = None
        for l in range(layers):
            if b + 2 <= nr:
                x = tiles[l, b * e:(b + 2) * e]
            else:
                x = jnp.concatenate([tiles[l, b * e:], halo[l]], axis=0)
            squares = x * x if squares is None else squares + x * x
            xh, xl = split(x)
            y = mm(row_left[...], jnp.concatenate([xh, xh, xl], axis=0))
            h, low = split(y)
            yh[b, l], yl[b, l] = h, low
        sh, sl = split(squares)
        energy = mm(band_left[...], jnp.concatenate([sh, sl], axis=0))
        eh, el = split(energy)
        for c in range(nc):
            width = min(2, nc - c) * e
            at = slice(c * e, c * e + width)
            window = mm(eh[:, at], band_right[:width]) + mm(el[:, at], band_right[:width])
            inv[b, :, c * e:(c + 1) * e] = 1.0 / jnp.sqrt(window / entries + 1e-05)

    for k in range(count):
        peaks[k:k + 1] = jnp.full((1, e), -jnp.inf, F32)

    def row_block(b, carry):
        for c in range(nc):
            width = min(2, nc - c) * e
            at = slice(c * e, c * e + width)
            tile_parts = []
            for l in range(layers):
                h, low = yh[b, l, :, at], yl[b, l, :, at]
                y = mm(h, col_right[0, :width]) + mm(low, col_right[0, :width]) + mm(h, col_right[1, :width])
                tile_parts.append(combine(y, e))
            for k in range(count):
                u1 = u2 = v1 = v2 = None
                for l in range(layers):
                    p1, p2, q1, q2 = tile_parts[l]
                    c1, c2, d1, d2 = (spectra[k, l, n] for n in range(4))
                    t = (p1 * c1 + p2 * c2, p2 * c1 - p1 * c2, q1 * d1 + q2 * d2, q2 * d1 - q1 * d2)
                    if u1 is None:
                        u1, u2, v1, v2 = t
                    else:
                        u1, u2, v1, v2 = u1 + t[0], u2 + t[1], v1 + t[2], v2 + t[3]
                z = jnp.concatenate([
                    jnp.concatenate([u1 + v1, u2 - v2], axis=1),
                    jnp.concatenate([u2 + v2, v1 - u1], axis=1)], axis=0)
                zh, zl = split(z)
                w = mm(zh, back_right[0]) + mm(zl, back_right[0]) + mm(zh, back_right[1])
                h, low = split(w)
                wh[k, :, c * e:(c + 1) * e] = h
                wl[k, :, c * e:(c + 1) * e] = low
        scale = inv[b]
        for k in range(count):
            out = mm(back_left[...], jnp.concatenate([wh[k], wh[k], wl[k]], axis=0))
            out = out * scale * (clip_scale[k] * 0.5)
            scores[k // per_block, k % per_block, pl.ds(pl.multiple_of(b * e, e), e)] = out
            top = jnp.max(out, axis=0, keepdims=True)
            best = peaks[k:k + 1]
            for c in range(nc):
                best = jnp.maximum(best, top[:, c * e:(c + 1) * e])
            peaks[k:k + 1] = best
        return carry

    lax.fori_loop(0, nr, row_block, 0)


def correlate(tiles, halo, clips, order):
    layers, rows, cols = tiles.shape
    blocks, per_block = clips.shape[:2]
    e = clips.shape[-1]
    span = 2 * e
    nr = rows // e
    count = blocks * per_block
    vmem = pl.BlockSpec(memory_space=pltpu.VMEM)
    return pl.pallas_call(
        kernel,
        out_shape=(jax.ShapeDtypeStruct((blocks, per_block, rows, cols), F32),
                   jax.ShapeDtypeStruct((count, e), F32)),
        in_specs=[pl.BlockSpec(memory_space=pltpu.SMEM)] + [vmem] * 9,
        out_specs=(vmem, vmem),
        scratch_shapes=[
            pltpu.VMEM((nr, layers, span, cols), BF16),
            pltpu.VMEM((nr, layers, span, cols), BF16),
            pltpu.VMEM((nr, e, cols), F32),
            pltpu.VMEM((count, layers, 4, e, e), F32),
            pltpu.VMEM((count, span, cols), BF16),
            pltpu.VMEM((count, span, cols), BF16),
        ],
        compiler_params=pltpu.CompilerParams(vmem_limit_bytes=60 * 1024 * 1024),
    )(order, tiles, halo, clips, *constants(e))


def local(tiles, library, block_owner, block_clips, layer_order):
    e = library.shape[-1]
    halo = from_behind(tiles[:, :e, :], "tile")
    picked = library[block_clips]
    owned = block_owner == lax.axis_index("tile")
    delivered = lax.psum(jnp.where(owned[:, None, None, None, None], picked, 0.0), "tile")
    scores, peaks = correlate(tiles, halo, delivered, layer_order)
    peak = lax.pmax(jnp.max(peaks, axis=1), "tile").reshape(block_clips.shape)
    return scores, peak


def solution(mesh):
    in_specs = (
        P(None, ("groups", "tile"), None),
        P("tile", None, None, None),
        P(),
        P(),
        P(("groups", "tile"), None),
    )
    out_specs = (P(None, None, ("groups", "tile"), None), P("groups", None))
    return jax.shard_map(local, mesh=mesh, in_specs=in_specs, out_specs=out_specs, check_vma=False)
```

```python
import functools
import math

import jax
import jax.numpy as jnp
import numpy as np
from jax import lax
from jax.experimental import pallas as pl
from jax.experimental.pallas import tpu as pltpu
from jax.sharding import PartitionSpec as P

F32 = jnp.float32
BF16 = jnp.bfloat16


def split(x):
    high = x.astype(BF16)
    return high, (x - high.astype(F32)).astype(BF16)


def mm(a, b):
    return jnp.dot(a, b, preferred_element_type=F32)


def transform_matrix(extent):
    span = 2 * extent
    odd = 2 * np.arange(extent)[:, None] + 1
    angle = (odd * np.arange(span)[None, :] % (2 * span)) * (math.pi / span)
    return np.concatenate([np.cos(angle), np.sin(angle)], axis=0).astype(np.float32)


def halves(matrix):
    high = matrix.astype(BF16)
    low = (matrix - high.astype(np.float32)).astype(BF16)
    return high, low


def constants(extent):
    forward = transform_matrix(extent)
    fh, fl = halves(forward)
    row_left = np.concatenate([fh, fl, fh], axis=1)
    ft = np.ascontiguousarray(forward.T)
    th, tl = halves(ft)
    col_right = np.stack([th, tl])
    back = forward[:, :extent] * np.float32(1.0 / extent)
    bh, bl = halves(back)
    back_right = np.stack([bh, bl])
    back_left = np.concatenate([bh.T, bl.T, bh.T], axis=1)
    offset = np.arange(2 * extent)[None, :] - np.arange(extent)[:, None]
    band = ((offset >= 0) & (offset < extent)).astype(BF16)
    band_left = np.concatenate([band, band], axis=1)
    band_right = np.ascontiguousarray(band.T)
    return [jnp.asarray(c) for c in (row_left, col_right, back_left, back_right, band_left, band_right)]


def combine(y, e):
    a, b = y[:e, :e], y[:e, e:]
    c, d = y[e:, :e], y[e:, e:]
    return a - d, b + c, a + d, c - b


def kernel(order, tiles, halo, clips, row_left, col_right, back_left, back_right, band_left, band_right,
           scores, peaks, yh, yl, inv, spectra, wh, wl):
    layers, rows, cols = tiles.shape
    blocks, per_block = clips.shape[:2]
    count = blocks * per_block
    e = clips.shape[-1]
    span = 2 * e
    nr, nc = rows // e, cols // e
    entries = layers * e * e

    clip_scale = []
    for k in range(count):
        total = jnp.zeros((e, e), F32)
        for l in range(layers):
            chosen = clips[k // per_block, k % per_block, order[0, l]]
            total = total + chosen * chosen
            ch, cl = split(chosen)
            first = mm(row_left[:, :e], ch) + mm(row_left[:, span:span + e], ch) + mm(row_left[:, :e], cl)
            fh, fl = split(first)
            second = mm(fh, col_right[0, :e]) + mm(fl, col_right[0, :e]) + mm(fh, col_right[1, :e])
            for n, part in enumerate(combine(second, e)):
                spectra[k, l, n] = part
        mean = jnp.sum(total, keepdims=True) / entries
        clip_scale.append(1.0 / (math.sqrt(entries) * jnp.sqrt(mean + 1e-05)))

    for b in range(nr):
        squares = None
        for l in range(layers):
            if b + 2 <= nr:
                x = tiles[l, b * e:(b + 2) * e]
            else:
                x = jnp.concatenate([tiles[l, b * e:], halo[l]], axis=0)
            squares = x * x if squares is None else squares + x * x
            xh, xl = split(x)
            y = mm(row_left[...], jnp.concatenate([xh, xh, xl], axis=0))
            h, low = split(y)
            yh[b, l], yl[b, l] = h, low
        sh, sl = split(squares)
        energy = mm(band_left[...], jnp.concatenate([sh, sl], axis=0))
        eh, el = split(energy)
        for c in range(nc):
            width = min(2, nc - c) * e
            at = slice(c * e, c * e + width)
            window = mm(eh[:, at], band_right[:width]) + mm(el[:, at], band_right[:width])
            inv[b, :, c * e:(c + 1) * e] = 1.0 / jnp.sqrt(window / entries + 1e-05)

    peaks[...] = jnp.full(peaks.shape, -jnp.inf, F32)

    def row_block(b, carry):
        for c in range(nc):
            width = min(2, nc - c) * e
            at = slice(c * e, c * e + width)
            tile_parts = []
            for l in range(layers):
                h, low = yh[b, l, :, at], yl[b, l, :, at]
                y = mm(h, col_right[0, :width]) + mm(low, col_right[0, :width]) + mm(h, col_right[1, :width])
                tile_parts.append(combine(y, e))
            for k in range(count):
                u1 = u2 = v1 = v2 = None
                for l in range(layers):
                    p1, p2, q1, q2 = tile_parts[l]
                    c1, c2, d1, d2 = (spectra[k, l, n] for n in range(4))
                    t = (p1 * c1 + p2 * c2, p2 * c1 - p1 * c2, q1 * d1 + q2 * d2, q2 * d1 - q1 * d2)
                    if u1 is None:
                        u1, u2, v1, v2 = t
                    else:
                        u1, u2, v1, v2 = u1 + t[0], u2 + t[1], v1 + t[2], v2 + t[3]
                z = jnp.concatenate([
                    jnp.concatenate([u1 + v1, u2 - v2], axis=1),
                    jnp.concatenate([u2 + v2, v1 - u1], axis=1)], axis=0)
                zh, zl = split(z)
                w = mm(zh, back_right[0]) + mm(zl, back_right[0]) + mm(zh, back_right[1])
                h, low = split(w)
                wh[k, :, c * e:(c + 1) * e] = h
                wl[k, :, c * e:(c + 1) * e] = low
        scale = inv[b]
        for k in range(count):
            out = mm(back_left[...], jnp.concatenate([wh[k], wh[k], wl[k]], axis=0))
            out = out * scale * (clip_scale[k] * 0.5)
            scores[k // per_block, k % per_block, pl.ds(pl.multiple_of(b * e, e), e)] = out
            top = jnp.max(out, axis=0, keepdims=True)
            best = peaks[k:k + 1]
            for c in range(nc):
                best = jnp.maximum(best, top[:, c * e:(c + 1) * e])
            peaks[k:k + 1] = best
        return carry

    lax.fori_loop(0, nr, row_block, 0)


def correlate(tiles, halo, clips, order):
    layers, rows, cols = tiles.shape
    blocks, per_block = clips.shape[:2]
    e = clips.shape[-1]
    span = 2 * e
    nr = rows // e
    count = blocks * per_block
    vmem = pl.BlockSpec(memory_space=pltpu.VMEM)
    return pl.pallas_call(
        kernel,
        out_shape=(jax.ShapeDtypeStruct((blocks, per_block, rows, cols), F32),
                   jax.ShapeDtypeStruct((-(-count // 8) * 8, e), F32)),
        in_specs=[pl.BlockSpec(memory_space=pltpu.SMEM)] + [vmem] * 9,
        out_specs=(vmem, vmem),
        scratch_shapes=[
            pltpu.VMEM((nr, layers, span, cols), BF16),
            pltpu.VMEM((nr, layers, span, cols), BF16),
            pltpu.VMEM((nr, e, cols), F32),
            pltpu.VMEM((count, layers, 4, e, e), F32),
            pltpu.VMEM((count, span, cols), BF16),
            pltpu.VMEM((count, span, cols), BF16),
        ],
        compiler_params=pltpu.CompilerParams(vmem_limit_bytes=60 * 1024 * 1024),
    )(order, tiles, halo, clips, *constants(e))


MESH = pl.DeviceIdType.MESH
PLANE = 4
CHUNKS = 4


def share_kernel(groups, tiles_n, owner, picks, library, tiles, full_out, halo_out,
                 stage, landed, mine, rbuf, lbuf, rsend, lsend, full, zeros,
                 rs_send, rs_recv, r_send, r_recv, l_send, l_recv,
                 ag_send, ag_recv, fw_send, fw_recv, halo_send, halo_recv, zero_sem):
    g = lax.axis_index("groups")
    t = lax.axis_index("tile")
    per_block = picks.shape[1]
    layers, e = library.shape[1], library.shape[-1]
    z = t // PLANE
    q = lax.rem(t, PLANE)
    depth = tiles_n // PLANE
    parity = lax.rem(g, 2)
    other_g = g + 1 - 2 * parity
    core = lax.rem(q, 2)
    partner = t + 1 - 2 * core
    upper = q // 2
    across = t + 2 - 4 * upper
    plane = [z * PLANE + lax.rem(q + d, PLANE) for d in range(1, PLANE)]
    always = [(g, other) for other in plane] + [(other_g, t), (other_g, across)]
    sometimes = [(z > 0, (g, t - PLANE)), (z < depth - 1, (g, t + PLANE)),
                 (t > 0, (g, t - 1)), (t < tiles_n - 1, (g, t + 1))]

    barrier = pltpu.get_barrier_semaphore()
    for target in always:
        pl.semaphore_signal(barrier, inc=1, device_id=target, device_id_type=MESH)
    for there, target in sometimes:
        @pl.when(there)
        def _(target=target):
            pl.semaphore_signal(barrier, inc=1, device_id=target, device_id_type=MESH)

    def contribution(slab):
        clip, layer = slab // layers, lax.rem(slab, layers)
        block, which = clip // per_block, lax.rem(clip, per_block)
        mask = jnp.where(owner[block] == t, 1.0, 0.0).astype(F32)
        return library[picks[block, which], layer] * mask

    for d in range(PLANE):
        stage[d] = contribution(parity * PLANE + lax.rem(q + d, PLANE))

    @pl.when(z == 0)
    def _():
        rbuf[...] = jnp.zeros_like(rbuf)

    @pl.when(z == depth - 1)
    def _():
        lbuf[...] = jnp.zeros_like(lbuf)

    pl.semaphore_wait(barrier, len(always) + sum(jnp.where(there, 1, 0) for there, _ in sometimes))

    def remote(src, dst, send, recv, target):
        return pltpu.make_async_remote_copy(src_ref=src, dst_ref=dst, send_sem=send, recv_sem=recv,
                                            device_id=target, device_id_type=MESH)

    scatter = []
    for d in range(1, PLANE):
        copy = remote(stage.at[d], landed.at[d - 1], rs_send.at[d - 1], rs_recv.at[d - 1], (g, plane[d - 1]))
        copy.start()
        scatter.append(copy)
    for copy in scatter:
        copy.wait()
    mine[...] = stage[0] + landed[0] + landed[1] + landed[2]

    halo = remote(tiles.at[:, pl.ds(0, e)], halo_out, halo_send, halo_recv, (g, t - 1))

    @pl.when(t > 0)
    def _():
        halo.start()

    @pl.when(t == tiles_n - 1)
    def _():
        zeros[...] = jnp.zeros_like(zeros)
        fill = pltpu.make_async_copy(zeros, halo_out, zero_sem)
        fill.start()
        fill.wait()

    step = e // CHUNKS
    parts = [pl.ds(c * step, step) for c in range(CHUNKS)]
    slab = parity * PLANE + q
    right = [remote(rsend.at[c], rbuf.at[c], r_send.at[c], r_recv.at[c], (g, t + PLANE)) for c in range(CHUNKS)]
    left = [remote(lsend.at[c], lbuf.at[c], l_send.at[c], l_recv.at[c], (g, t - PLANE)) for c in range(CHUNKS)]
    forwards = []
    slabs = [slab, (1 - parity) * PLANE + q,
             parity * PLANE + q + 2 - 4 * upper, (1 - parity) * PLANE + q + 2 - 4 * upper]
    targets = [(other_g, t), (g, across), (other_g, across)]

    def forward(n, c):
        copy = remote(full.at[slabs[n], parts[c]], full.at[slabs[n], parts[c]],
                      fw_send.at[n, c], fw_recv.at[n, c], (g, partner))
        copy.start()
        forwards.append(copy)

    gathers = [(n, c, remote(full.at[slab, parts[c]], full.at[slab, parts[c]], ag_send.at[n, c], ag_recv.at[n, c], target))
               for c in range(CHUNKS) for n, target in enumerate(targets)]
    own = [remote(full.at[slab, parts[c]], full.at[slab, parts[c]], fw_send.at[0, c], fw_recv.at[0, c], (g, partner))
           for c in range(CHUNKS)]

    def rightward(c):
        @pl.when(z > 0)
        def _():
            right[c].wait_recv()
        rsend[c] = rbuf[c] + mine[parts[c]]

        @pl.when(z < depth - 1)
        def _():
            right[c].start()

    def leftward(c):
        @pl.when(z < depth - 1)
        def _():
            left[c].wait_recv()
        lsend[c] = lbuf[c] + mine[parts[c]]

        @pl.when(z > 0)
        def _():
            left[c].start()

    def deliver(c):
        full[slab, parts[c]] = rsend[c] + lbuf[c]
        for n in range(3):
            gathers[3 * c + n][2].start()
        own[c].start()

    lower = z < depth // 2
    for condition, first, second in ((lower, rightward, leftward), (jnp.logical_not(lower), leftward, rightward)):
        @pl.when(condition)
        def _(first=first, second=second):
            for c in range(CHUNKS):
                first(c)
            for c in range(CHUNKS):
                second(c)
                deliver(c)
    forwards.extend(own)
    for n, c, copy in gathers:
        copy.wait_recv()
        forward(n + 1, c)
    for copy in forwards:
        copy.wait_recv()
    full_out[...] = full[...]
    for _, _, copy in gathers:
        copy.wait_send()
    for copy in forwards:
        copy.wait_send()
    for c in range(CHUNKS):
        @pl.when(z < depth - 1)
        def _(c=c):
            right[c].wait_send()

        @pl.when(z > 0)
        def _(c=c):
            left[c].wait_send()

    @pl.when(t > 0)
    def _():
        halo.wait_send()

    @pl.when(t < tiles_n - 1)
    def _():
        halo.wait_recv()


def share(tiles, library, block_owner, block_clips):
    layers, e = library.shape[1], library.shape[-1]
    cols = tiles.shape[-1]
    slabs = block_clips.size * layers
    assert slabs == 2 * PLANE
    groups, tiles_n = lax.axis_size("groups"), lax.axis_size("tile")
    smem = pl.BlockSpec(memory_space=pltpu.SMEM)
    vmem = pl.BlockSpec(memory_space=pltpu.VMEM)
    hbm = pl.BlockSpec(memory_space=pl.ANY)
    dma = pltpu.SemaphoreType.DMA
    piece = pltpu.VMEM((CHUNKS, e // CHUNKS, e), F32)
    return pl.pallas_call(
        functools.partial(share_kernel, groups, tiles_n),
        out_shape=(jax.ShapeDtypeStruct((slabs, e, e), F32), jax.ShapeDtypeStruct((layers, e, cols), F32)),
        in_specs=[smem, smem, vmem, hbm],
        out_specs=(vmem, hbm),
        scratch_shapes=[
            pltpu.VMEM((PLANE, e, e), F32), pltpu.VMEM((PLANE - 1, e, e), F32), pltpu.VMEM((e, e), F32),
            piece, piece, piece, piece,
            pltpu.VMEM((slabs, e, e), F32), pltpu.VMEM((layers, e, cols), F32),
            dma((PLANE - 1,)), dma((PLANE - 1,)), dma((CHUNKS,)), dma((CHUNKS,)), dma((CHUNKS,)), dma((CHUNKS,)),
            dma((3, CHUNKS)), dma((3, CHUNKS)), dma((4, CHUNKS)), dma((4, CHUNKS)), dma, dma, dma,
        ],
        compiler_params=pltpu.CompilerParams(collective_id=0, has_side_effects=True),
    )(block_owner, block_clips, library, tiles)


def peak_kernel(tiles_n, per_block, peaks, out, slots, send, recv):
    g = lax.axis_index("groups")
    t = lax.axis_index("tile")
    others = [(g, lax.rem(t + d, tiles_n)) for d in range(1, tiles_n)]
    barrier = pltpu.get_barrier_semaphore()
    for target in others:
        pl.semaphore_signal(barrier, inc=1, device_id=target, device_id_type=MESH)
    pl.semaphore_wait(barrier, tiles_n - 1)
    copies = []
    for n, target in enumerate(others):
        copy = pltpu.make_async_remote_copy(src_ref=peaks, dst_ref=slots.at[n], send_sem=send.at[n],
                                            recv_sem=recv.at[n], device_id=target, device_id_type=MESH)
        copy.start()
        copies.append(copy)
    best = peaks[...]
    for n, copy in enumerate(copies):
        copy.wait_recv()
        best = jnp.maximum(best, slots[n])
    best = jnp.max(best, axis=1, keepdims=True)
    for k in range(out.shape[0] * per_block):
        at = k % per_block
        out[k // per_block:k // per_block + 1, at:at + 1] = best[k:k + 1]
    for copy in copies:
        copy.wait_send()


def share_peaks(peaks, shape):
    tiles_n = lax.axis_size("tile")
    vmem = pl.BlockSpec(memory_space=pltpu.VMEM)
    dma = pltpu.SemaphoreType.DMA
    return pl.pallas_call(
        functools.partial(peak_kernel, tiles_n, shape[1]),
        out_shape=jax.ShapeDtypeStruct(shape, F32),
        in_specs=[vmem],
        out_specs=vmem,
        scratch_shapes=[pltpu.VMEM((tiles_n - 1,) + peaks.shape, F32), dma((tiles_n - 1,)), dma((tiles_n - 1,))],
        compiler_params=pltpu.CompilerParams(collective_id=1, has_side_effects=True),
    )(peaks)


def local(tiles, library, block_owner, block_clips, layer_order):
    layers, e = library.shape[1], library.shape[-1]
    delivered, halo = share(tiles, library, block_owner, block_clips)
    clips = delivered.reshape(block_clips.shape + (layers, e, e))
    scores, peaks = correlate(tiles, halo, clips, layer_order)
    return scores, share_peaks(peaks, block_clips.shape)


def solution(mesh):
    in_specs = (
        P(None, ("groups", "tile"), None),
        P("tile", None, None, None),
        P(),
        P(),
        P(("groups", "tile"), None),
    )
    out_specs = (P(None, None, ("groups", "tile"), None), P("groups", None))
    return jax.shard_map(local, mesh=mesh, in_specs=in_specs, out_specs=out_specs, check_vma=False)
```

```python
import functools
import math

import jax
import jax.numpy as jnp
import numpy as np
from jax import lax
from jax.experimental import pallas as pl
from jax.experimental.pallas import tpu as pltpu
from jax.sharding import PartitionSpec as P

F32 = jnp.float32
BF16 = jnp.bfloat16


def split(x):
    high = x.astype(BF16)
    return high, (x - high.astype(F32)).astype(BF16)


def mm(a, b):
    return jnp.dot(a, b, preferred_element_type=F32)


def transform_matrix(extent):
    span = 2 * extent
    odd = 2 * np.arange(extent)[:, None] + 1
    angle = (odd * np.arange(span)[None, :] % (2 * span)) * (math.pi / span)
    return np.concatenate([np.cos(angle), np.sin(angle)], axis=0).astype(np.float32)


def halves(matrix):
    high = matrix.astype(BF16)
    low = (matrix - high.astype(np.float32)).astype(BF16)
    return high, low


def constants(extent):
    forward = transform_matrix(extent)
    fh, fl = halves(forward)
    row_left = np.concatenate([fh, fl, fh], axis=1)
    ft = np.ascontiguousarray(forward.T)
    th, tl = halves(ft)
    col_right = np.stack([th, tl])
    back = forward[:, :extent] * np.float32(1.0 / extent)
    bh, bl = halves(back)
    back_right = np.stack([bh, bl])
    back_left = np.concatenate([bh.T, bl.T, bh.T], axis=1)
    offset = np.arange(2 * extent)[None, :] - np.arange(extent)[:, None]
    band = ((offset >= 0) & (offset < extent)).astype(BF16)
    band_left = np.concatenate([band, band], axis=1)
    band_right = np.ascontiguousarray(band.T)
    return [jnp.asarray(c) for c in (row_left, col_right, back_left, back_right, band_left, band_right)]


def combine(y, e):
    a, b = y[:e, :e], y[:e, e:]
    c, d = y[e:, :e], y[e:, e:]
    return a - d, b + c, a + d, c - b


class Transforms:
    def __init__(self, refs, shapes):
        self.__dict__.update(refs)
        self.layers, self.rows, self.cols, self.e, self.per_block, self.count = shapes
        self.span = 2 * self.e
        self.nc = self.cols // self.e
        self.entries = self.layers * self.e * self.e

    def rows_of(self, b, window):
        e, squares = self.e, None
        for l in range(self.layers):
            x = window(l)
            squares = x * x if squares is None else squares + x * x
            xh, xl = split(x)
            y = mm(self.row_left[...], jnp.concatenate([xh, xh, xl], axis=0))
            h, low = split(y)
            self.yh[l], self.yl[l] = h, low
        sh, sl = split(squares)
        energy = mm(self.band_left[...], jnp.concatenate([sh, sl], axis=0))
        eh, el = split(energy)
        for c in range(self.nc):
            width = min(2, self.nc - c) * e
            at = slice(c * e, c * e + width)
            total = mm(eh[:, at], self.band_right[:width]) + mm(el[:, at], self.band_right[:width])
            self.inv[b, :, c * e:(c + 1) * e] = 1.0 / jnp.sqrt(total / self.entries + 1e-05)

    def columns_of(self, b):
        e = self.e
        for c in range(self.nc):
            width = min(2, self.nc - c) * e
            at = slice(c * e, c * e + width)
            for l in range(self.layers):
                h, low = self.yh[l, :, at], self.yl[l, :, at]
                y = mm(h, self.col_right[0, :width]) + mm(low, self.col_right[0, :width]) + mm(h, self.col_right[1, :width])
                for n, part in enumerate(combine(y, e)):
                    self.tile_parts[b, c, l, n] = part

    def clip_of(self, k, layer_at):
        e, span, row_left, col_right = self.e, self.span, self.row_left, self.col_right
        total = jnp.zeros((e, e), F32)
        for l in range(self.layers):
            chosen = layer_at(l)
            total = total + chosen * chosen
            ch, cl = split(chosen)
            first = mm(row_left[:, :e], ch) + mm(row_left[:, span:span + e], ch) + mm(row_left[:, :e], cl)
            fh, fl = split(first)
            second = mm(fh, col_right[0, :e]) + mm(fl, col_right[0, :e]) + mm(fh, col_right[1, :e])
            for n, part in enumerate(combine(second, e)):
                self.spectra[k, l, n] = part
        mean = jnp.sum(total, keepdims=True) / self.entries
        return 1.0 / (math.sqrt(self.entries) * jnp.sqrt(mean + 1e-05))

    def inverse_of(self, b, clip_scale):
        e = self.e
        for c in range(self.nc):
            for k in range(self.count):
                u1 = u2 = v1 = v2 = None
                for l in range(self.layers):
                    p1, p2, q1, q2 = (self.tile_parts[b, c, l, n] for n in range(4))
                    c1, c2, d1, d2 = (self.spectra[k, l, n] for n in range(4))
                    t = (p1 * c1 + p2 * c2, p2 * c1 - p1 * c2, q1 * d1 + q2 * d2, q2 * d1 - q1 * d2)
                    if u1 is None:
                        u1, u2, v1, v2 = t
                    else:
                        u1, u2, v1, v2 = u1 + t[0], u2 + t[1], v1 + t[2], v2 + t[3]
                z = jnp.concatenate([
                    jnp.concatenate([u1 + v1, u2 - v2], axis=1),
                    jnp.concatenate([u2 + v2, v1 - u1], axis=1)], axis=0)
                zh, zl = split(z)
                w = mm(zh, self.back_right[0]) + mm(zl, self.back_right[0]) + mm(zh, self.back_right[1])
                h, low = split(w)
                self.wh[k, :, c * e:(c + 1) * e] = h
                self.wl[k, :, c * e:(c + 1) * e] = low
        scale = self.inv[b]
        for k in range(self.count):
            out = mm(self.back_left[...], jnp.concatenate([self.wh[k], self.wh[k], self.wl[k]], axis=0))
            out = out * scale * (clip_scale[k] * 0.5)
            self.scores[k // self.per_block, k % self.per_block, pl.ds(pl.multiple_of(b * e, e), e)] = out
            top = jnp.max(out, axis=0, keepdims=True)
            best = self.peaks[k:k + 1]
            for c in range(self.nc):
                best = jnp.maximum(best, top[:, c * e:(c + 1) * e])
            self.peaks[k:k + 1] = best


MESH = pl.DeviceIdType.MESH
PLANE = 4
CHUNKS = 4


def kernel(tiles_n, owner, picks, order, library, tiles, row_left, col_right, back_left, back_right,
           band_left, band_right, scores, peak_out,
           yh, yl, inv, tile_parts, spectra, wh, wl, peaks, slots,
           stage, landed, mine, rbuf, lbuf, rsend, lsend, full, halo_in,
           rs_send, rs_recv, r_send, r_recv, l_send, l_recv,
           ag_send, ag_recv, fw_send, fw_recv, halo_send, halo_recv, peak_send, peak_recv):
    g = lax.axis_index("groups")
    t = lax.axis_index("tile")
    per_block = picks.shape[1]
    layers, rows, cols = tiles.shape
    e = library.shape[-1]
    nr = rows // e
    count = picks.shape[0] * per_block
    work = Transforms(dict(row_left=row_left, col_right=col_right, back_left=back_left, back_right=back_right,
                           band_left=band_left, band_right=band_right, scores=scores, yh=yh, yl=yl, inv=inv,
                           tile_parts=tile_parts, spectra=spectra, wh=wh, wl=wl, peaks=peaks),
                      (layers, rows, cols, e, per_block, count))
    z = t // PLANE
    q = lax.rem(t, PLANE)
    depth = tiles_n // PLANE
    parity = lax.rem(g, 2)
    other_g = g + 1 - 2 * parity
    core = lax.rem(q, 2)
    partner = t + 1 - 2 * core
    upper = q // 2
    across = t + 2 - 4 * upper
    plane = [z * PLANE + lax.rem(q + d, PLANE) for d in range(1, PLANE)]
    others = [(g, lax.rem(t + d, tiles_n)) for d in range(1, tiles_n)]
    greeted = others + [(other_g, t), (other_g, across)]

    barrier = pltpu.get_barrier_semaphore()
    for target in greeted:
        pl.semaphore_signal(barrier, inc=1, device_id=target, device_id_type=MESH)

    def contribution(slab):
        clip, layer = slab // layers, lax.rem(slab, layers)
        block, which = clip // per_block, lax.rem(clip, per_block)
        mask = jnp.where(owner[block] == t, 1.0, 0.0).astype(F32)
        return library[picks[block, which], layer] * mask

    for d in range(PLANE):
        stage[d] = contribution(parity * PLANE + lax.rem(q + d, PLANE))

    @pl.when(z == 0)
    def _():
        rbuf[...] = jnp.zeros_like(rbuf)

    @pl.when(z == depth - 1)
    def _():
        lbuf[...] = jnp.zeros_like(lbuf)

    @pl.when(t == tiles_n - 1)
    def _():
        halo_in[...] = jnp.zeros_like(halo_in)

    peaks[...] = jnp.full(peaks.shape, -jnp.inf, F32)
    pl.semaphore_wait(barrier, len(greeted))

    def remote(src, dst, send, recv, target):
        return pltpu.make_async_remote_copy(src_ref=src, dst_ref=dst, send_sem=send, recv_sem=recv,
                                            device_id=target, device_id_type=MESH)

    scatter = []
    for d in range(1, PLANE):
        copy = remote(stage.at[d], landed.at[d - 1], rs_send.at[d - 1], rs_recv.at[d - 1], (g, plane[d - 1]))
        copy.start()
        scatter.append(copy)
    work.rows_of(0, lambda l: tiles[l, :2 * e])
    for copy in scatter:
        copy.wait()
    mine[...] = stage[0] + landed[0] + landed[1] + landed[2]

    step = e // CHUNKS
    parts = [pl.ds(c * step, step) for c in range(CHUNKS)]
    slab = parity * PLANE + q
    right = [remote(rsend.at[c], rbuf.at[c], r_send.at[c], r_recv.at[c], (g, t + PLANE)) for c in range(CHUNKS)]
    left = [remote(lsend.at[c], lbuf.at[c], l_send.at[c], l_recv.at[c], (g, t - PLANE)) for c in range(CHUNKS)]
    forwards = []
    slabs = [slab, (1 - parity) * PLANE + q,
             parity * PLANE + q + 2 - 4 * upper, (1 - parity) * PLANE + q + 2 - 4 * upper]
    targets = [(other_g, t), (g, across), (other_g, across)]

    def forward(n, c):
        copy = remote(full.at[slabs[n], parts[c]], full.at[slabs[n], parts[c]],
                      fw_send.at[n, c], fw_recv.at[n, c], (g, partner))
        copy.start()
        forwards.append(copy)

    gathers = [(n, c, remote(full.at[slab, parts[c]], full.at[slab, parts[c]], ag_send.at[n, c], ag_recv.at[n, c], target))
               for c in range(CHUNKS) for n, target in enumerate(targets)]
    own = [remote(full.at[slab, parts[c]], full.at[slab, parts[c]], fw_send.at[0, c], fw_recv.at[0, c], (g, partner))
           for c in range(CHUNKS)]

    def rightward(c):
        @pl.when(z > 0)
        def _():
            right[c].wait_recv()
        rsend[c] = rbuf[c] + mine[parts[c]]

        @pl.when(z < depth - 1)
        def _():
            right[c].start()

    def leftward(c):
        @pl.when(z < depth - 1)
        def _():
            left[c].wait_recv()
        lsend[c] = lbuf[c] + mine[parts[c]]

        @pl.when(z > 0)
        def _():
            left[c].start()

    def deliver(c):
        full[slab, parts[c]] = rsend[c] + lbuf[c]
        for n in range(3):
            gathers[3 * c + n][2].start()
        own[c].start()

    lower = z < depth // 2
    for condition, first, second in ((lower, rightward, leftward), (jnp.logical_not(lower), leftward, rightward)):
        @pl.when(condition)
        def _(first=first, second=second):
            for c in range(CHUNKS):
                first(c)
            for c in range(CHUNKS):
                second(c)
                deliver(c)
    forwards.extend(own)
    work.columns_of(0)
    work.rows_of(1, lambda l: tiles[l, e:3 * e])
    for n, c, copy in gathers:
        copy.wait_recv()
        forward(n + 1, c)
    halo = remote(tiles.at[:, pl.ds(0, e)], halo_in, halo_send, halo_recv, (g, t - 1))

    @pl.when(t > 0)
    def _():
        halo.start()

    for b in range(1, nr - 1):
        if b > 1:
            work.rows_of(b, lambda l: tiles[l, b * e:(b + 2) * e])
        work.columns_of(b)
    for copy in forwards:
        copy.wait_recv()
    clip_scale = [work.clip_of(k, lambda l: full[k * layers + order[0, l]]) for k in range(count)]

    def row_block(b, carry):
        @pl.when(b == nr - 1)
        def _():
            @pl.when(t < tiles_n - 1)
            def _():
                halo.wait_recv()
            work.rows_of(nr - 1, lambda l: jnp.concatenate([tiles[l, rows - e:], halo_in[l]], axis=0))
            work.columns_of(nr - 1)
        work.inverse_of(b, clip_scale)
        return carry

    lax.fori_loop(0, nr, row_block, 0)

    copies = [remote(peaks, slots.at[n], peak_send.at[n], peak_recv.at[n], target) for n, target in enumerate(others)]
    for copy in copies:
        copy.start()
    for _, _, copy in gathers:
        copy.wait_send()
    for copy in forwards:
        copy.wait_send()
    for c in range(CHUNKS):
        @pl.when(z < depth - 1)
        def _(c=c):
            right[c].wait_send()

        @pl.when(z > 0)
        def _(c=c):
            left[c].wait_send()

    @pl.when(t > 0)
    def _():
        halo.wait_send()

    best = peaks[...]
    for n, copy in enumerate(copies):
        copy.wait_recv()
        best = jnp.maximum(best, slots[n])
    best = jnp.max(best, axis=1, keepdims=True)
    for k in range(count):
        at = k % per_block
        peak_out[k // per_block:k // per_block + 1, at:at + 1] = best[k:k + 1]
    for copy in copies:
        copy.wait_send()


def local(tiles, library, block_owner, block_clips, layer_order):
    layers, rows, cols = tiles.shape
    e = library.shape[-1]
    span, nr, nc = 2 * e, rows // e, cols // e
    blocks, per_block = block_clips.shape
    count = blocks * per_block
    slabs = count * layers
    assert slabs == 2 * PLANE
    tiles_n = lax.axis_size("tile")
    smem = pl.BlockSpec(memory_space=pltpu.SMEM)
    vmem = pl.BlockSpec(memory_space=pltpu.VMEM)
    dma = pltpu.SemaphoreType.DMA
    piece = pltpu.VMEM((CHUNKS, e // CHUNKS, e), F32)
    lines = -(-count // 8) * 8
    return pl.pallas_call(
        functools.partial(kernel, tiles_n),
        out_shape=(jax.ShapeDtypeStruct((blocks, per_block, rows, cols), F32),
                   jax.ShapeDtypeStruct((blocks, per_block), F32)),
        in_specs=[smem] * 3 + [vmem] * 8,
        out_specs=(vmem, vmem),
        scratch_shapes=[
            pltpu.VMEM((layers, span, cols), BF16), pltpu.VMEM((layers, span, cols), BF16),
            pltpu.VMEM((nr, e, cols), F32),
            pltpu.VMEM((nr, nc, layers, 4, e, e), F32), pltpu.VMEM((count, layers, 4, e, e), F32),
            pltpu.VMEM((count, span, cols), BF16), pltpu.VMEM((count, span, cols), BF16),
            pltpu.VMEM((lines, e), F32), pltpu.VMEM((tiles_n - 1, lines, e), F32),
            pltpu.VMEM((PLANE, e, e), F32), pltpu.VMEM((PLANE - 1, e, e), F32), pltpu.VMEM((e, e), F32),
            piece, piece, piece, piece,
            pltpu.VMEM((slabs, e, e), F32), pltpu.VMEM((layers, e, cols), F32),
            dma((PLANE - 1,)), dma((PLANE - 1,)), dma((CHUNKS,)), dma((CHUNKS,)), dma((CHUNKS,)), dma((CHUNKS,)),
            dma((3, CHUNKS)), dma((3, CHUNKS)), dma((4, CHUNKS)), dma((4, CHUNKS)), dma, dma,
            dma((tiles_n - 1,)), dma((tiles_n - 1,)),
        ],
        compiler_params=pltpu.CompilerParams(collective_id=0, has_side_effects=True, vmem_limit_bytes=60 * 1024 * 1024),
    )(block_owner, block_clips, layer_order, library, tiles, *constants(e))


def solution(mesh):
    in_specs = (
        P(None, ("groups", "tile"), None),
        P("tile", None, None, None),
        P(),
        P(),
        P(("groups", "tile"), None),
    )
    out_specs = (P(None, None, ("groups", "tile"), None), P("groups", None))
    return jax.shard_map(local, mesh=mesh, in_specs=in_specs, out_specs=out_specs, check_vma=False)
```

```python
import functools
import math

import jax
import jax.numpy as jnp
import numpy as np
from jax import lax
from jax.experimental import pallas as pl
from jax.experimental.pallas import tpu as pltpu
from jax.sharding import PartitionSpec as P

F32 = jnp.float32
BF16 = jnp.bfloat16


def split(x):
    high = x.astype(BF16)
    return high, (x - high.astype(F32)).astype(BF16)


def mm(a, b):
    return jnp.dot(a, b, preferred_element_type=F32)


def transform_matrix(extent):
    span = 2 * extent
    odd = 2 * np.arange(extent)[:, None] + 1
    angle = (odd * np.arange(span)[None, :] % (2 * span)) * (math.pi / span)
    return np.concatenate([np.cos(angle), np.sin(angle)], axis=0).astype(np.float32)


def halves(matrix):
    high = matrix.astype(BF16)
    low = (matrix - high.astype(np.float32)).astype(BF16)
    return high, low


def constants(extent):
    forward = transform_matrix(extent)
    fh, fl = halves(forward)
    row_left = np.concatenate([fh, fl, fh], axis=1)
    ft = np.ascontiguousarray(forward.T)
    th, tl = halves(ft)
    col_right = np.stack([th, tl])
    back = forward[:, :extent] * np.float32(1.0 / extent)
    bh, bl = halves(back)
    back_right = np.stack([bh, bl])
    back_left = np.concatenate([bh.T, bl.T, bh.T], axis=1)
    offset = np.arange(2 * extent)[None, :] - np.arange(extent)[:, None]
    band = ((offset >= 0) & (offset < extent)).astype(BF16)
    band_left = np.concatenate([band, band], axis=1)
    band_right = np.ascontiguousarray(band.T)
    return [jnp.asarray(c) for c in (row_left, col_right, back_left, back_right, band_left, band_right)]


def combine(y, e):
    a, b = y[:e, :e], y[:e, e:]
    c, d = y[e:, :e], y[e:, e:]
    return a - d, b + c, a + d, c - b


class Transforms:
    def __init__(self, refs, shapes):
        self.__dict__.update(refs)
        self.layers, self.rows, self.cols, self.e, self.per_block, self.count = shapes
        self.span = 2 * self.e
        self.nc = self.cols // self.e
        self.entries = self.layers * self.e * self.e

    def rows_of(self, b, window):
        e, squares = self.e, None
        for l in range(self.layers):
            x = window(l)
            squares = x * x if squares is None else squares + x * x
            xh, xl = split(x)
            y = mm(self.row_left[...], jnp.concatenate([xh, xh, xl], axis=0))
            h, low = split(y)
            self.yh[l], self.yl[l] = h, low
        sh, sl = split(squares)
        energy = mm(self.band_left[...], jnp.concatenate([sh, sl], axis=0))
        eh, el = split(energy)
        for c in range(self.nc):
            width = min(2, self.nc - c) * e
            at = slice(c * e, c * e + width)
            total = mm(eh[:, at], self.band_right[:width]) + mm(el[:, at], self.band_right[:width])
            self.inv[b, :, c * e:(c + 1) * e] = 1.0 / jnp.sqrt(total / self.entries + 1e-05)

    def columns_of(self, b):
        e = self.e
        for c in range(self.nc):
            width = min(2, self.nc - c) * e
            at = slice(c * e, c * e + width)
            for l in range(self.layers):
                h, low = self.yh[l, :, at], self.yl[l, :, at]
                y = mm(h, self.col_right[0, :width]) + mm(low, self.col_right[0, :width]) + mm(h, self.col_right[1, :width])
                for n, part in enumerate(combine(y, e)):
                    self.tile_parts[b, c, l, n] = part

    def clip_of(self, k, layer_at):
        e, span, row_left, col_right = self.e, self.span, self.row_left, self.col_right
        total = jnp.zeros((e, e), F32)
        for l in range(self.layers):
            chosen = layer_at(l)
            total = total + chosen * chosen
            ch, cl = split(chosen)
            first = mm(row_left[:, :e], ch) + mm(row_left[:, span:span + e], ch) + mm(row_left[:, :e], cl)
            fh, fl = split(first)
            second = mm(fh, col_right[0, :e]) + mm(fl, col_right[0, :e]) + mm(fh, col_right[1, :e])
            for n, part in enumerate(combine(second, e)):
                self.spectra[k, l, n] = part
        mean = jnp.sum(total, keepdims=True) / self.entries
        return 1.0 / (math.sqrt(self.entries) * jnp.sqrt(mean + 1e-05))

    def inverse_of(self, b, clip_scale):
        e = self.e
        for c in range(self.nc):
            for k in range(self.count):
                u1 = u2 = v1 = v2 = None
                for l in range(self.layers):
                    p1, p2, q1, q2 = (self.tile_parts[b, c, l, n] for n in range(4))
                    c1, c2, d1, d2 = (self.spectra[k, l, n] for n in range(4))
                    t = (p1 * c1 + p2 * c2, p2 * c1 - p1 * c2, q1 * d1 + q2 * d2, q2 * d1 - q1 * d2)
                    if u1 is None:
                        u1, u2, v1, v2 = t
                    else:
                        u1, u2, v1, v2 = u1 + t[0], u2 + t[1], v1 + t[2], v2 + t[3]
                z = jnp.concatenate([
                    jnp.concatenate([u1 + v1, u2 - v2], axis=1),
                    jnp.concatenate([u2 + v2, v1 - u1], axis=1)], axis=0)
                zh, zl = split(z)
                w = mm(zh, self.back_right[0]) + mm(zl, self.back_right[0]) + mm(zh, self.back_right[1])
                h, low = split(w)
                self.wh[k, :, c * e:(c + 1) * e] = h
                self.wl[k, :, c * e:(c + 1) * e] = low
        scale = self.inv[b]
        for k in range(self.count):
            out = mm(self.back_left[...], jnp.concatenate([self.wh[k], self.wh[k], self.wl[k]], axis=0))
            out = out * scale * (clip_scale[k] * 0.5)
            self.scores[k // self.per_block, k % self.per_block, pl.ds(pl.multiple_of(b * e, e), e)] = out
            top = jnp.max(out, axis=0, keepdims=True)
            best = self.peaks[k:k + 1]
            for c in range(self.nc):
                best = jnp.maximum(best, top[:, c * e:(c + 1) * e])
            self.peaks[k:k + 1] = best


MESH = pl.DeviceIdType.MESH
PLANE = 4
CHUNKS = 4


def kernel(tiles_n, owner, picks, order, *refs):
    sources = refs[:8]
    (scores, peak_out,
           yh, yl, inv, tile_parts, spectra, wh, wl, peaks, slots,
           stage, landed, mine, rbuf, lbuf, rsend, lsend, full, halo_in,
           rs_send, rs_recv, r_send, r_recv, l_send, l_recv,
           ag_send, ag_recv, fw_send, fw_recv, halo_send, halo_recv, peak_send, peak_recv,
           library, tiles, row_left, col_right, back_left, back_right, band_left, band_right, load_sem) = refs[8:]
    loads = [pltpu.make_async_copy(a, b, load_sem.at[n]) for n, (a, b) in enumerate(zip(
        sources, (library, tiles, row_left, col_right, back_left, back_right, band_left, band_right)))]
    for load in loads:
        load.start()
    g = lax.axis_index("groups")
    t = lax.axis_index("tile")
    per_block = picks.shape[1]
    layers, rows, cols = tiles.shape
    e = library.shape[-1]
    nr = rows // e
    count = picks.shape[0] * per_block
    work = Transforms(dict(row_left=row_left, col_right=col_right, back_left=back_left, back_right=back_right,
                           band_left=band_left, band_right=band_right, scores=scores, yh=yh, yl=yl, inv=inv,
                           tile_parts=tile_parts, spectra=spectra, wh=wh, wl=wl, peaks=peaks),
                      (layers, rows, cols, e, per_block, count))
    z = t // PLANE
    q = lax.rem(t, PLANE)
    depth = tiles_n // PLANE
    parity = lax.rem(g, 2)
    other_g = g + 1 - 2 * parity
    core = lax.rem(q, 2)
    partner = t + 1 - 2 * core
    upper = q // 2
    across = t + 2 - 4 * upper
    plane = [z * PLANE + lax.rem(q + d, PLANE) for d in range(1, PLANE)]
    others = [(g, lax.rem(t + d, tiles_n)) for d in range(1, tiles_n)]
    greeted = others + [(other_g, t), (other_g, across)]

    barrier = pltpu.get_barrier_semaphore()
    for target in greeted:
        pl.semaphore_signal(barrier, inc=1, device_id=target, device_id_type=MESH)

    loads[0].wait()

    def contribution(slab):
        clip, layer = slab // layers, lax.rem(slab, layers)
        block, which = clip // per_block, lax.rem(clip, per_block)
        mask = jnp.where(owner[block] == t, 1.0, 0.0).astype(F32)
        return library[picks[block, which], layer] * mask

    for d in range(PLANE):
        stage[d] = contribution(parity * PLANE + lax.rem(q + d, PLANE))

    @pl.when(z == 0)
    def _():
        rbuf[...] = jnp.zeros_like(rbuf)

    @pl.when(z == depth - 1)
    def _():
        lbuf[...] = jnp.zeros_like(lbuf)

    @pl.when(t == tiles_n - 1)
    def _():
        halo_in[...] = jnp.zeros_like(halo_in)

    peaks[...] = jnp.full(peaks.shape, -jnp.inf, F32)
    pl.semaphore_wait(barrier, len(greeted))

    def remote(src, dst, send, recv, target):
        return pltpu.make_async_remote_copy(src_ref=src, dst_ref=dst, send_sem=send, recv_sem=recv,
                                            device_id=target, device_id_type=MESH)

    scatter = []
    for d in range(1, PLANE):
        copy = remote(stage.at[d], landed.at[d - 1], rs_send.at[d - 1], rs_recv.at[d - 1], (g, plane[d - 1]))
        copy.start()
        scatter.append(copy)
    for load in loads[1:]:
        load.wait()
    work.rows_of(0, lambda l: tiles[l, :2 * e])
    for copy in scatter:
        copy.wait()
    mine[...] = stage[0] + landed[0] + landed[1] + landed[2]

    step = e // CHUNKS
    parts = [pl.ds(c * step, step) for c in range(CHUNKS)]
    slab = parity * PLANE + q
    right = [remote(rsend.at[c], rbuf.at[c], r_send.at[c], r_recv.at[c], (g, t + PLANE)) for c in range(CHUNKS)]
    left = [remote(lsend.at[c], lbuf.at[c], l_send.at[c], l_recv.at[c], (g, t - PLANE)) for c in range(CHUNKS)]
    forwards = []
    slabs = [slab, (1 - parity) * PLANE + q,
             parity * PLANE + q + 2 - 4 * upper, (1 - parity) * PLANE + q + 2 - 4 * upper]
    targets = [(other_g, t), (g, across), (other_g, across)]

    def forward(n, c):
        copy = remote(full.at[slabs[n], parts[c]], full.at[slabs[n], parts[c]],
                      fw_send.at[n, c], fw_recv.at[n, c], (g, partner))
        copy.start()
        forwards.append(copy)

    gathers = [(n, c, remote(full.at[slab, parts[c]], full.at[slab, parts[c]], ag_send.at[n, c], ag_recv.at[n, c], target))
               for c in range(CHUNKS) for n, target in enumerate(targets)]
    own = [remote(full.at[slab, parts[c]], full.at[slab, parts[c]], fw_send.at[0, c], fw_recv.at[0, c], (g, partner))
           for c in range(CHUNKS)]

    def rightward(c):
        @pl.when(z > 0)
        def _():
            right[c].wait_recv()
        rsend[c] = rbuf[c] + mine[parts[c]]

        @pl.when(z < depth - 1)
        def _():
            right[c].start()

    def leftward(c):
        @pl.when(z < depth - 1)
        def _():
            left[c].wait_recv()
        lsend[c] = lbuf[c] + mine[parts[c]]

        @pl.when(z > 0)
        def _():
            left[c].start()

    def deliver(c):
        full[slab, parts[c]] = rsend[c] + lbuf[c]
        for n in range(3):
            gathers[3 * c + n][2].start()
        own[c].start()

    lower = z < depth // 2
    for condition, first, second in ((lower, rightward, leftward), (jnp.logical_not(lower), leftward, rightward)):
        @pl.when(condition)
        def _(first=first, second=second):
            for c in range(CHUNKS):
                first(c)
            for c in range(CHUNKS):
                second(c)
                deliver(c)
    forwards.extend(own)
    work.columns_of(0)
    work.rows_of(1, lambda l: tiles[l, e:3 * e])
    for n, c, copy in gathers:
        copy.wait_recv()
        forward(n + 1, c)
    halo = remote(tiles.at[:, pl.ds(0, e)], halo_in, halo_send, halo_recv, (g, t - 1))

    @pl.when(t > 0)
    def _():
        halo.start()

    for b in range(1, nr - 1):
        if b > 1:
            work.rows_of(b, lambda l: tiles[l, b * e:(b + 2) * e])
        work.columns_of(b)
    for copy in forwards:
        copy.wait_recv()
    clip_scale = [work.clip_of(k, lambda l: full[k * layers + order[0, l]]) for k in range(count)]

    def row_block(b, carry):
        @pl.when(b == nr - 1)
        def _():
            @pl.when(t < tiles_n - 1)
            def _():
                halo.wait_recv()
            work.rows_of(nr - 1, lambda l: jnp.concatenate([tiles[l, rows - e:], halo_in[l]], axis=0))
            work.columns_of(nr - 1)
        work.inverse_of(b, clip_scale)
        return carry

    lax.fori_loop(0, nr, row_block, 0)

    copies = [remote(peaks, slots.at[n], peak_send.at[n], peak_recv.at[n], target) for n, target in enumerate(others)]
    for copy in copies:
        copy.start()
    for _, _, copy in gathers:
        copy.wait_send()
    for copy in forwards:
        copy.wait_send()
    for c in range(CHUNKS):
        @pl.when(z < depth - 1)
        def _(c=c):
            right[c].wait_send()

        @pl.when(z > 0)
        def _(c=c):
            left[c].wait_send()

    @pl.when(t > 0)
    def _():
        halo.wait_send()

    best = peaks[...]
    for n, copy in enumerate(copies):
        copy.wait_recv()
        best = jnp.maximum(best, slots[n])
    best = jnp.max(best, axis=1, keepdims=True)
    for k in range(count):
        at = k % per_block
        peak_out[k // per_block:k // per_block + 1, at:at + 1] = best[k:k + 1]
    for copy in copies:
        copy.wait_send()


def local(tiles, library, block_owner, block_clips, layer_order):
    layers, rows, cols = tiles.shape
    e = library.shape[-1]
    span, nr, nc = 2 * e, rows // e, cols // e
    blocks, per_block = block_clips.shape
    count = blocks * per_block
    slabs = count * layers
    assert slabs == 2 * PLANE
    tiles_n = lax.axis_size("tile")
    smem = pl.BlockSpec(memory_space=pltpu.SMEM)
    vmem = pl.BlockSpec(memory_space=pltpu.VMEM)
    dma = pltpu.SemaphoreType.DMA
    piece = pltpu.VMEM((CHUNKS, e // CHUNKS, e), F32)
    lines = -(-count // 8) * 8
    operands = [library, tiles, *constants(e)]
    return pl.pallas_call(
        functools.partial(kernel, tiles_n),
        out_shape=(jax.ShapeDtypeStruct((blocks, per_block, rows, cols), F32),
                   jax.ShapeDtypeStruct((blocks, per_block), F32)),
        in_specs=[smem] * 3 + [pl.BlockSpec(memory_space=pltpu.HBM)] * 8,
        out_specs=(vmem, vmem),
        scratch_shapes=[
            pltpu.VMEM((layers, span, cols), BF16), pltpu.VMEM((layers, span, cols), BF16),
            pltpu.VMEM((nr, e, cols), F32),
            pltpu.VMEM((nr, nc, layers, 4, e, e), F32), pltpu.VMEM((count, layers, 4, e, e), F32),
            pltpu.VMEM((count, span, cols), BF16), pltpu.VMEM((count, span, cols), BF16),
            pltpu.VMEM((lines, e), F32), pltpu.VMEM((tiles_n - 1, lines, e), F32),
            pltpu.VMEM((PLANE, e, e), F32), pltpu.VMEM((PLANE - 1, e, e), F32), pltpu.VMEM((e, e), F32),
            piece, piece, piece, piece,
            pltpu.VMEM((slabs, e, e), F32), pltpu.VMEM((layers, e, cols), F32),
            dma((PLANE - 1,)), dma((PLANE - 1,)), dma((CHUNKS,)), dma((CHUNKS,)), dma((CHUNKS,)), dma((CHUNKS,)),
            dma((3, CHUNKS)), dma((3, CHUNKS)), dma((4, CHUNKS)), dma((4, CHUNKS)), dma, dma,
            dma((tiles_n - 1,)), dma((tiles_n - 1,)),
        ] + [pltpu.VMEM(a.shape, a.dtype) for a in operands] + [dma((len(operands),))],
        compiler_params=pltpu.CompilerParams(collective_id=0, has_side_effects=True, vmem_limit_bytes=60 * 1024 * 1024),
    )(block_owner, block_clips, layer_order, *operands)


def solution(mesh):
    in_specs = (
        P(None, ("groups", "tile"), None),
        P("tile", None, None, None),
        P(),
        P(),
        P(("groups", "tile"), None),
    )
    out_specs = (P(None, None, ("groups", "tile"), None), P("groups", None))
    return jax.shard_map(local, mesh=mesh, in_specs=in_specs, out_specs=out_specs, check_vma=False)
```
